32 devices in a mesh: row: 8 (over z, y), col: 4 (over x, core).
Axes of the slice: x: 2, y: 2, z: 4, core: 2. Of those that a mesh axis runs over, the one named last changes fastest.
Arguments:
- vectors: bfloat16 [16384, 256], P(('row', 'col'))
- tile_values: bfloat16 [8, 4, 80, 256, 256], P('row', 'col')
- tile_row: int32 [8, 4, 80], P('row', 'col'), may hold values from 0 to 7, as said below
- tile_col: int32 [8, 4, 80], P('row', 'col'), may hold values from 0 to 15, as said below
- counts: int32 [8, 4], P('row', 'col'), may hold values from 40 to 80, as said below
Outputs:
- basis: float32 [16384, 256], P(('row', 'col'))
- factor: float32 [256, 256], replicated
The draws below stay inside these ranges and needn't reach their ends.
Inputs may be any that keep to these rules, and one draw needn't show every extreme that they name: Within one device the pairs (tile_row, tile_col) of its slots are distinct, and every tile row of a block row has a slot on every device below counts. `tile_col`: column index of a slot's tile within the device's column set. `counts`: some device fills all 80 slots in every draw.
All inputs are finite; a program needn't handle non-finite values.
Results may differ from the reference program's by a relative error of at most 0.0003.
Values may be sent and summed in bfloat16 or wider, within the bound.
A program may use at most 128 MiB of HBM per device.

```python
import math
import jax
import jax.numpy as jnp
from jax import lax

K = 256
TB = 256
S = 512
TILES = 80
TROWS = 8
TCOLS = 16
NROWS = 16384
N_ROW = 8
N_COL = 4


def tile_pattern(key):
    devices_all = N_ROW * N_COL
    base = jax.random.fold_in(key, 4242)
    row_keys = jax.random.split(jax.random.fold_in(base, 1), devices_all)
    row_perms = jax.vmap(lambda single: jax.random.permutation(single, TROWS))(row_keys)
    col_keys = jax.random.split(jax.random.fold_in(base, 2), devices_all * TROWS)
    col_perms = jax.vmap(lambda single: jax.random.permutation(single, TCOLS))(col_keys)
    col_perms = col_perms.reshape(devices_all, TROWS, TCOLS)
    slots = jnp.arange(TILES, dtype=jnp.int32)
    member = slots % TROWS
    layer = slots // TROWS
    rows_out = row_perms[:, member]
    cols_out = col_perms[:, member, layer]
    return (rows_out.reshape(N_ROW, N_COL, TILES).astype(jnp.int32), cols_out.reshape(N_ROW, N_COL, TILES).astype(jnp.int32))


def draw_tile_row(key, part):
    return tile_pattern(key)[0]


def draw_tile_col(key, part):
    return tile_pattern(key)[1]


def draw_counts(key, part):
    devices_all = N_ROW * N_COL
    first, second, third = jax.random.split(key, 3)
    values = jax.random.randint(first, (devices_all,), TILES // 2, TILES + 1)
    fullest = jax.random.randint(second, (), 0, devices_all)
    emptiest = (fullest + 1 + jax.random.randint(third, (), 0, devices_all - 1)) % devices_all
    index = jnp.arange(devices_all)
    values = jnp.where(index == fullest, TILES, values)
    values = jnp.where(index == emptiest, TILES // 2, values)
    return values.reshape(N_ROW, N_COL).astype(jnp.int32)


def draw_vectors(key, part):
    first = jax.random.fold_in(key, 17)
    values = jax.random.normal(first, (NROWS, K), jnp.float32)
    return values.astype(jnp.bfloat16)


def draw_tile_values(key, part):
    first, second = jax.random.split(key)
    shape = (N_ROW, N_COL, TILES, TB, TB)
    trend = jnp.sqrt(1.0 + 2.0 * jnp.arange(N_ROW, dtype=jnp.float32) / (N_ROW - 1))
    values = jax.random.normal(first, shape, jnp.float32)
    row_scale = jnp.exp(jax.random.uniform(second, (N_ROW, N_COL, TILES, TB, 1), jnp.float32, math.log(0.3), math.log(3.0)))
    values = values * row_scale * trend[:, None, None, None, None] / math.sqrt(4.0 * TB)
    return values.astype(jnp.bfloat16)


def setup_inputs(seed: int = 0) -> dict:
    splits = jax.random.split(jax.random.key(seed), 6)
    vectors = draw_vectors(jax.random.fold_in(splits[5], 71), 0)
    tile_values = draw_tile_values(jax.random.fold_in(splits[5], 71), 0)
    tile_row = draw_tile_row(jax.random.fold_in(splits[5], 71), 0)
    tile_col = draw_tile_col(jax.random.fold_in(splits[5], 71), 0)
    counts = draw_counts(jax.random.fold_in(splits[5], 71), 0)
    return {"vectors": vectors, "tile_values": tile_values, "tile_row": tile_row, "tile_col": tile_col, "counts": counts}


def reference(vectors, tile_values, tile_row, tile_col, counts):
    grid = vectors.reshape(N_ROW, N_COL, S, K)
    slots = jnp.arange(TILES, dtype=jnp.int32)

    def block_row(rindex):

        def one_column(cindex):
            column_set = lax.dynamic_index_in_dim(grid, cindex, axis=1, keepdims=False)
            column_set = column_set.reshape(TCOLS, TB, K)
            picked = column_set[tile_col[rindex, cindex]]
            tiles = tile_values[rindex, cindex].astype(jnp.float32)
            prods = jnp.einsum('tij,tjk->tik', tiles, picked.astype(jnp.float32))
            valid = (slots < counts[rindex, cindex]).astype(jnp.float32)
            prods = prods * valid[:, None, None]
            return jax.ops.segment_sum(prods, tile_row[rindex, cindex], num_segments=TROWS)
        parts = lax.map(one_column, jnp.arange(N_COL, dtype=jnp.int32))
        return jnp.sum(parts, axis=0)
    panel = lax.map(block_row, jnp.arange(N_ROW, dtype=jnp.int32)).reshape(NROWS, K)
    gram = jnp.dot(panel.T, panel, precision=lax.Precision.HIGHEST) / NROWS
    lower = jnp.linalg.cholesky(gram)
    basis = jax.scipy.linalg.solve_triangular(lower, panel.T, lower=True).T
    return (basis, lower.T)
```

```python
import functools

import jax
import jax.numpy as jnp
from jax import lax
from jax.experimental import pallas as pl
from jax.experimental.pallas import tpu as pltpu
from jax.sharding import PartitionSpec as P

MESH = pl.DeviceIdType.MESH
HIGH = lax.Precision.HIGHEST
TILE_DMAS = 8
RS_CHUNKS = 4
CHOL_BLOCK = 32
GROUP = 8


def split_row_axis(n):
    y = 1
    while (2 * y) * (2 * y) <= n:
        y *= 2
    return n // y, y


def nearest(k, at, n):
    low = jnp.minimum(at, n - 1 - at)
    near = jnp.where(k % 2 == 1, at - (k + 1) // 2, at + k // 2)
    rest = jnp.where(at < n - 1 - at, k, n - 1 - k)
    return jnp.where(k <= 2 * low, near, rest)


def panel_kernel(
    n_row, n_col, table, vectors, tiles, panel, gram,
    vbuf, tbuf, acc, r1, r2, gpart, grecv, gfull,
    tile_sem, own_sem, ag_send, ag_recv, s1_send, s1_recv, s2_send, s2_recv,
    g_send, g_recv, f_send, f_recv,
):
    n_dev = n_row * n_col
    nz, ny = split_row_axis(n_row)
    nx = n_col // 2
    row = lax.axis_index("row")
    col = lax.axis_index("col")
    me = row * n_col + col
    z, y = row // ny, row % ny
    x, core = col // 2, col % 2
    slab, width = vectors.shape
    slots, block, _ = tiles.shape
    per_block = slab // block
    tile_rows = n_col * per_block
    tile_cols = n_row * per_block
    owners, own_rows, _ = gfull.shape

    own_copy = pltpu.make_async_copy(vectors, vbuf.at[row], own_sem)
    own_copy.start()
    per_dma = slots // TILE_DMAS
    tile_copies = [
        pltpu.make_async_copy(
            tiles.at[pl.ds(i * per_dma, per_dma)],
            tbuf.at[pl.ds(i * per_dma, per_dma)],
            tile_sem.at[i],
        )
        for i in range(TILE_DMAS)
    ]

    barrier = pltpu.get_barrier_semaphore()

    def greet(j, carry):
        peer = (me + j) % n_dev
        pl.semaphore_signal(
            barrier, inc=1, device_id=(peer // n_col, peer % n_col), device_id_type=MESH
        )
        return carry

    lax.fori_loop(1, n_dev, greet, 0)
    for copy in tile_copies:
        copy.start()
    tbuf[slots] = jnp.zeros((block, block), tbuf.dtype)
    acc[...] = jnp.zeros_like(acc)
    own_copy.wait()
    pl.semaphore_wait(barrier, n_dev - 1)

    def hop(way, b, to_row):
        return pltpu.make_async_remote_copy(
            src_ref=vbuf.at[b], dst_ref=vbuf.at[b],
            send_sem=ag_send.at[way, b], recv_sem=ag_recv.at[b],
            device_id=(to_row, col), device_id_type=MESH,
        )

    def hops(b):
        bz, by = b // ny, b % ny
        same = by == y
        return (
            (same & (bz <= z) & (z + 1 < nz), hop(0, b, jnp.minimum(row + ny, n_row - 1))),
            (same & (bz >= z) & (z >= 1), hop(1, b, jnp.maximum(row - ny, 0))),
            ((by <= y) & (y + 1 < ny), hop(2, b, jnp.minimum(row + 1, n_row - 1))),
            ((by >= y) & (y >= 1), hop(3, b, jnp.maximum(row - 1, 0))),
        )

    def gather_step(i, carry):
        b = nearest(i // ny, z, nz) * ny + nearest(i % ny, y, ny)

        @pl.when(i > 0)
        def _():
            hop(0, b, row).wait_recv()

        for needed, copy in hops(b):
            @pl.when(needed)
            def _(copy=copy):
                copy.start()

        @pl.when(i == 0)
        def _():
            for copy in tile_copies:
                copy.wait()

        for r in range(tile_rows):
            total = None
            for c in range(per_block):
                slot = table[r * tile_cols + b * per_block + c]
                part = jnp.dot(
                    tbuf[slot],
                    vbuf[b, pl.ds(c * block, block), :],
                    preferred_element_type=jnp.float32,
                )
                total = part if total is None else total + part
            rows = pl.ds(r % per_block * block, block)
            acc[r // per_block, rows, :] += total
        return carry

    lax.fori_loop(0, n_row, gather_step, 0)

    piece = slab // RS_CHUNKS

    def to_partner(xp, h):
        rows = pl.ds(h * piece, piece)
        return pltpu.make_async_remote_copy(
            src_ref=acc.at[xp * 2 + 1 - core, rows], dst_ref=r1.at[xp, rows],
            send_sem=s1_send.at[xp, h], recv_sem=s1_recv.at[xp, h],
            device_id=(row, x * 2 + 1 - core), device_id_type=MESH,
        )

    def across(xp, h):
        rows = pl.ds(h * piece, piece)
        return pltpu.make_async_remote_copy(
            src_ref=acc.at[xp * 2 + core, rows], dst_ref=r2.at[x, rows],
            send_sem=s2_send.at[xp, h], recv_sem=s2_recv.at[x, h],
            device_id=(row, xp * 2 + core), device_id_type=MESH,
        )

    def from_across(xp, h):
        rows = pl.ds(h * piece, piece)
        return pltpu.make_async_remote_copy(
            src_ref=acc.at[xp * 2 + core, rows], dst_ref=r2.at[xp, rows],
            send_sem=s2_send.at[xp, h], recv_sem=s2_recv.at[xp, h],
            device_id=(row, xp * 2 + core), device_id_type=MESH,
        )

    order = [(x + 1 + i) % nx for i in range(nx)]
    for xp in order:
        for h in range(RS_CHUNKS):
            to_partner(xp, h).start()
    for i, xp in enumerate(order):
        for h in range(RS_CHUNKS):
            rows = pl.ds(h * piece, piece)
            to_partner(xp, h).wait_recv()
            acc[xp * 2 + core, rows, :] += r1[xp, rows, :]
            if i < nx - 1:
                across(xp, h).start()
    local = None
    for h in range(RS_CHUNKS):
        rows = pl.ds(h * piece, piece)
        value = acc[x * 2 + core, rows, :]
        for xp in order[:-1]:
            from_across(xp, h).wait_recv()
            value = value + r2[xp, rows, :]
        panel[rows, :] = value
        part = lax.dot_general(
            value, value, (((0,), (0,)), ((), ())),
            precision=HIGH, preferred_element_type=jnp.float32,
        )
        local = part if local is None else local + part
    gpart[...] = (local / (slab * n_dev)).reshape(owners, own_rows, width)

    def to_owner(o):
        return pltpu.make_async_remote_copy(
            src_ref=gpart.at[o], dst_ref=grecv.at[me],
            send_sem=g_send.at[o], recv_sem=g_recv.at[me],
            device_id=(o // n_col, o % n_col), device_id_type=MESH,
        )

    def from_member(s):
        return pltpu.make_async_remote_copy(
            src_ref=gpart.at[0], dst_ref=grecv.at[s],
            send_sem=g_send.at[0], recv_sem=g_recv.at[s],
            device_id=(s // n_col, s % n_col), device_id_type=MESH,
        )

    def spread(o, s):
        return pltpu.make_async_remote_copy(
            src_ref=gfull.at[o], dst_ref=gfull.at[o],
            send_sem=f_send.at[s], recv_sem=f_recv.at[o],
            device_id=(s // n_col, s % n_col), device_id_type=MESH,
        )

    def each_peer(fn):
        def step(j, carry):
            fn((me + j) % n_dev)
            return carry
        lax.fori_loop(1, n_dev, step, 0)

    def each_owner(fn):
        def checked(o):
            if owners == n_dev:
                fn(o)
            else:
                @pl.when(o < owners)
                def _():
                    fn(o)
        each_peer(checked)

    def if_owner(fn):
        if owners == n_dev:
            fn()
        else:
            pl.when(me < owners)(fn)

    each_owner(lambda o: to_owner(o).start())

    def reduce_mine():
        grecv[me] = gpart[me]
        each_peer(lambda s: from_member(s).wait_recv())
        gfull[me] = jnp.sum(grecv[...], axis=0)
        each_peer(lambda s: spread(me, s).start())

    if_owner(reduce_mine)
    each_owner(lambda o: spread(o, me).wait_recv())
    gram[...] = gfull[...].reshape(width, width)

    each_owner(lambda o: to_owner(o).wait_send())
    if_owner(lambda: each_peer(lambda s: spread(me, s).wait_send()))
    for xp in order:
        for h in range(RS_CHUNKS):
            to_partner(xp, h).wait_send()
    for xp in order[:-1]:
        for h in range(RS_CHUNKS):
            across(xp, h).wait_send()

    def drain(b, carry):
        for needed, copy in hops(b):
            @pl.when(needed)
            def _(copy=copy):
                copy.wait_send()
        return carry

    lax.fori_loop(0, n_row, drain, 0)


def invert_factor(diag):
    n = diag.shape[0]
    lanes = 128
    rows = lax.broadcasted_iota(jnp.int32, (n, lanes), 0)
    cols = lax.broadcasted_iota(jnp.int32, (n, lanes), 1)
    eye = (cols - n == rows).astype(jnp.float32)
    work = jnp.concatenate([diag, eye[:, n:]], axis=1)
    scale = jnp.zeros((n, lanes), jnp.float32)
    for start in range(0, n, GROUP):
        picked = [
            jnp.broadcast_to(work[:, start + j : start + j + 1], (n, lanes))
            for j in range(GROUP)
        ]
        for j in range(GROUP):
            at = start + j
            pivot = picked[j][at : at + 1, :]
            scale = jnp.where(rows == at, lax.rsqrt(pivot), scale)
            weight = jnp.where(rows > at, picked[j] * (1.0 / pivot), 0.0)
            for later in range(j + 1, GROUP):
                picked[later] = picked[later] - weight * picked[later][at : at + 1, :]
            work = work - weight * work[at : at + 1, :]
    return (work * scale)[:, n : 2 * n]


def factor_kernel(gram, panel, basis, upper, work):
    width = gram.shape[0]
    n = CHOL_BLOCK
    rows = lax.broadcasted_iota(jnp.int32, (width, width), 0)
    cols = lax.broadcasted_iota(jnp.int32, (width, width), 1)
    work[:, :width] = gram[...]
    work[:, width:] = (rows == cols).astype(jnp.float32)
    for start in range(0, width, n):
        stop = start + n
        inverse = invert_factor(work[start:stop, start:stop])
        done = jnp.dot(
            inverse, work[start:stop, :], precision=HIGH, preferred_element_type=jnp.float32
        )
        work[start:stop, :] = done
        if stop < width:
            work[stop:, :] -= lax.dot_general(
                done[:, stop:width], done, (((0,), (0,)), ((), ())),
                precision=HIGH, preferred_element_type=jnp.float32,
            )
    upper[...] = jnp.where(cols >= rows, work[:, :width], 0.0)
    basis[...] = lax.dot_general(
        panel[...], work[:, width:], (((1,), (1,)), ((), ())),
        precision=HIGH, preferred_element_type=jnp.float32,
    )


def on_device(n_row, n_col, vectors, tile_values, tile_row, tile_col, counts):
    slab, width = vectors.shape
    tiles = tile_values[0, 0]
    slots, block, _ = tiles.shape
    n_dev = n_row * n_col
    per_block = slab // block
    tile_rows, tile_cols = n_col * per_block, n_row * per_block
    number = jnp.arange(slots, dtype=jnp.int32)
    place = tile_row[0, 0] * tile_cols + tile_col[0, 0]
    place = jnp.where(number < counts[0, 0], place, -1)
    cell = jnp.arange(tile_rows * tile_cols, dtype=jnp.int32)
    table = jnp.min(jnp.where(cell[:, None] == place[None, :], number[None, :], slots), axis=1)
    own_rows = max(8, width // n_dev)
    owners = width // own_rows
    nx = n_col // 2
    vmem = pl.BlockSpec(memory_space=pltpu.VMEM)
    f32 = jnp.float32
    panel, gram = pl.pallas_call(
        functools.partial(panel_kernel, n_row, n_col),
        out_shape=(
            jax.ShapeDtypeStruct((slab, width), f32),
            jax.ShapeDtypeStruct((width, width), f32),
        ),
        in_specs=[
            pl.BlockSpec(memory_space=pltpu.SMEM),
            pl.BlockSpec(memory_space=pl.ANY),
            pl.BlockSpec(memory_space=pl.ANY),
        ],
        out_specs=(vmem, vmem),
        scratch_shapes=[
            pltpu.VMEM((n_row, slab, width), vectors.dtype),
            pltpu.VMEM((slots + 1, block, block), tiles.dtype),
            pltpu.VMEM((n_col, slab, width), f32),
            pltpu.VMEM((nx, slab, width), f32),
            pltpu.VMEM((nx, slab, width), f32),
            pltpu.VMEM((owners, own_rows, width), f32),
            pltpu.VMEM((n_dev, own_rows, width), f32),
            pltpu.VMEM((owners, own_rows, width), f32),
            pltpu.SemaphoreType.DMA((TILE_DMAS,)),
            pltpu.SemaphoreType.DMA,
            pltpu.SemaphoreType.DMA((4, n_row)),
            pltpu.SemaphoreType.DMA((n_row,)),
            pltpu.SemaphoreType.DMA((nx, RS_CHUNKS)),
            pltpu.SemaphoreType.DMA((nx, RS_CHUNKS)),
            pltpu.SemaphoreType.DMA((nx, RS_CHUNKS)),
            pltpu.SemaphoreType.DMA((nx, RS_CHUNKS)),
            pltpu.SemaphoreType.DMA((owners,)),
            pltpu.SemaphoreType.DMA((n_dev,)),
            pltpu.SemaphoreType.DMA((n_dev,)),
            pltpu.SemaphoreType.DMA((owners,)),
        ],
        compiler_params=pltpu.CompilerParams(
            collective_id=0, has_side_effects=True, vmem_limit_bytes=56 << 20
        ),
        name="panel",
    )(table, vectors, tiles)
    basis, upper = pl.pallas_call(
        factor_kernel,
        out_shape=(
            jax.ShapeDtypeStruct((slab, width), f32),
            jax.ShapeDtypeStruct((width, width), f32),
        ),
        in_specs=[vmem, vmem],
        out_specs=(vmem, vmem),
        scratch_shapes=[pltpu.VMEM((width, 2 * width), f32)],
        name="factor",
    )(gram, panel)
    return (basis, upper)


def solution(mesh):
    n_row, n_col = mesh.shape["row"], mesh.shape["col"]
    return jax.shard_map(
        functools.partial(on_device, n_row, n_col),
        mesh=mesh,
        in_specs=(
            P(("row", "col"), None),
            P("row", "col", None, None, None),
            P("row", "col", None),
            P("row", "col", None),
            P("row", "col"),
        ),
        out_specs=(P(("row", "col"), None), P()),
        check_vma=False,
    )
```

```python
import functools

import jax
import jax.numpy as jnp
from jax import lax
from jax.experimental import pallas as pl
from jax.experimental.pallas import tpu as pltpu
from jax.sharding import PartitionSpec as P

MESH = pl.DeviceIdType.MESH
HIGH = lax.Precision.HIGHEST
TILE_DMAS = 8
RS_CHUNKS = 4
CHOL_BLOCK = 64
GROUP = 16


def split_row_axis(n):
    y = 1
    while (2 * y) * (2 * y) <= n:
        y *= 2
    return n // y, y


def nearest(k, at, n):
    low = jnp.minimum(at, n - 1 - at)
    near = jnp.where(k % 2 == 1, at - (k + 1) // 2, at + k // 2)
    rest = jnp.where(at < n - 1 - at, k, n - 1 - k)
    return jnp.where(k <= 2 * low, near, rest)


def visit(i, z, y, nz, ny):
    if ny == 2 and nz > 1:
        last = i == nz * ny - 1
        along = (i % 2 == 1) & ~last
        k = jnp.where(along, (i + 1) // 2, i // 2 - 1)
        k = jnp.where(i == 0, 0, jnp.where(last, nz - 1, k))
        j = jnp.where(along | (i == 0), 0, 1)
    else:
        k, j = i // ny, i % ny
    return nearest(k, z, nz) * ny + nearest(j, y, ny)


def panel_kernel(
    n_row, n_col, table, vectors, tiles, panel, gram,
    vbuf, tbuf, acc, r1, r2, gpart, grecv, gfull,
    tile_sem, own_sem, ag_send, ag_recv, s1_send, s1_recv, s2_send, s2_recv,
    g_send, g_recv, f_send, f_recv,
):
    n_dev = n_row * n_col
    nz, ny = split_row_axis(n_row)
    nx = n_col // 2
    row = lax.axis_index("row")
    col = lax.axis_index("col")
    me = row * n_col + col
    z, y = row // ny, row % ny
    x, core = col // 2, col % 2
    slab, width = vectors.shape
    slots, block, _ = tiles.shape
    half = width // 2
    per_block = slab // block
    tile_rows = n_col * per_block
    tile_cols = n_row * per_block
    pieces = gfull.shape[0]
    passes = grecv.shape[0]

    own_copies = [
        pltpu.make_async_copy(
            vectors.at[:, pl.ds(k * half, half)], vbuf.at[k, row], own_sem.at[k]
        )
        for k in range(2)
    ]
    for copy in own_copies:
        copy.start()
    per_dma = slots // TILE_DMAS
    tile_copies = [
        pltpu.make_async_copy(
            tiles.at[pl.ds(i * per_dma, per_dma)],
            tbuf.at[pl.ds(i * per_dma, per_dma)],
            tile_sem.at[i],
        )
        for i in range(TILE_DMAS)
    ]

    barrier = pltpu.get_barrier_semaphore()

    def greet(j, carry):
        peer = (me + j) % n_dev
        pl.semaphore_signal(
            barrier, inc=1, device_id=(peer // n_col, peer % n_col), device_id_type=MESH
        )
        return carry

    lax.fori_loop(1, n_dev, greet, 0)
    for copy in tile_copies:
        copy.start()
    tbuf[slots] = jnp.zeros((block, block), tbuf.dtype)
    acc[...] = jnp.zeros_like(acc)
    for copy in own_copies:
        copy.wait()
    pl.semaphore_wait(barrier, n_dev - 1)

    def hop(way, k, b, to_row):
        return pltpu.make_async_remote_copy(
            src_ref=vbuf.at[k, b], dst_ref=vbuf.at[k, b],
            send_sem=ag_send.at[way, k, b], recv_sem=ag_recv.at[k, b],
            device_id=(to_row, col), device_id_type=MESH,
        )

    def hops(k, b):
        bz, by = b // ny, b % ny
        same = by == y
        return (
            (same & (bz <= z) & (z + 1 < nz), hop(0, k, b, jnp.minimum(row + ny, n_row - 1))),
            (same & (bz >= z) & (z >= 1), hop(1, k, b, jnp.maximum(row - ny, 0))),
            ((by <= y) & (y + 1 < ny), hop(2, k, b, jnp.minimum(row + 1, n_row - 1))),
            ((by >= y) & (y >= 1), hop(3, k, b, jnp.maximum(row - 1, 0))),
        )

    def pass_on(k, b):
        for needed, copy in hops(k, b):
            @pl.when(needed)
            def _(copy=copy):
                copy.start()

    piece = slab // RS_CHUNKS
    order = [(x + 1 + i) % nx for i in range(nx)]

    def to_partner(k, xp, h):
        rows = pl.ds(h * piece, piece)
        return pltpu.make_async_remote_copy(
            src_ref=acc.at[k, xp * 2 + 1 - core, rows], dst_ref=r1.at[k, xp, rows],
            send_sem=s1_send.at[k, xp, h], recv_sem=s1_recv.at[k, xp, h],
            device_id=(row, x * 2 + 1 - core), device_id_type=MESH,
        )

    def across(k, xp, h, slot):
        rows = pl.ds(h * piece, piece)
        return pltpu.make_async_remote_copy(
            src_ref=acc.at[k, xp * 2 + core, rows], dst_ref=r2.at[k, slot, rows],
            send_sem=s2_send.at[k, xp, h], recv_sem=s2_recv.at[k, slot, h],
            device_id=(row, xp * 2 + core), device_id_type=MESH,
        )

    def give(k):
        for xp in order:
            for h in range(RS_CHUNKS):
                to_partner(k, xp, h).start()

    def take(k):
        for i, xp in enumerate(order):
            for h in range(RS_CHUNKS):
                rows = pl.ds(h * piece, piece)
                to_partner(k, xp, h).wait_recv()
                acc[k, xp * 2 + core, rows, :] += r1[k, xp, rows, :]
                if i < nx - 1:
                    across(k, xp, h, x).start()

    def finish(k, h):
        rows = pl.ds(h * piece, piece)
        value = acc[k, x * 2 + core, rows, :]
        for xp in order[:-1]:
            across(k, xp, h, xp).wait_recv()
            value = value + r2[k, xp, rows, :]
        panel[rows, k * half : (k + 1) * half] = value
        return value

    pass_on(0, row)

    def gather_step(i, carry):
        k, s = i // n_row, i % n_row
        b = visit(s, z, y, nz, ny)

        @pl.when(s > 0)
        def _():
            hop(0, k, b, row).wait_recv()
            pass_on(k, b)

        @pl.when(i == n_row // 2)
        def _():
            pass_on(1, row)

        @pl.when(i == 0)
        def _():
            for copy in tile_copies:
                copy.wait()

        for r in range(tile_rows):
            total = None
            for c in range(per_block):
                slot = table[r * tile_cols + b * per_block + c]
                part = jnp.dot(
                    tbuf[slot],
                    vbuf[k, b, pl.ds(c * block, block), :],
                    preferred_element_type=jnp.float32,
                )
                total = part if total is None else total + part
            rows = pl.ds(r % per_block * block, block)
            acc[k, r // per_block, rows, :] += total

        @pl.when(i == n_row - 1)
        def _():
            give(0)

        @pl.when(i == n_row + 1)
        def _():
            take(0)

        return carry

    lax.fori_loop(0, 2 * n_row, gather_step, 0)

    give(1)
    take(1)

    def gram_part(a, b):
        return lax.dot_general(
            a, b, (((0,), (0,)), ((), ())),
            precision=HIGH, preferred_element_type=jnp.float32,
        )

    g00 = g01 = g11 = jnp.zeros((half, half), jnp.float32)
    for h in range(RS_CHUNKS):
        value = finish(0, h)
        g00 = g00 + gram_part(value, value)
    for h in range(RS_CHUNKS):
        value = finish(1, h)
        g01 = g01 + gram_part(panel[pl.ds(h * piece, piece), :half], value)
        g11 = g11 + gram_part(value, value)

    total_rows = slab * n_dev
    rows = lax.broadcasted_iota(jnp.int32, (half, half), 0)
    cols = lax.broadcasted_iota(jnp.int32, (half, half), 1)
    each = half // 8
    gpart[0:each] = (g01 / total_rows).reshape(each, 8, half)
    gpart[each : 2 * each] = (jnp.where(rows > cols, g00, g11) / total_rows).reshape(each, 8, half)
    diagonal = jnp.sum(jnp.where(rows == cols, g00, 0.0), axis=0, keepdims=True)
    gpart[2 * each] = jnp.broadcast_to(diagonal / total_rows, (8, half))

    def to_owner(p, o):
        t = p * n_dev + o
        return pltpu.make_async_remote_copy(
            src_ref=gpart.at[t], dst_ref=grecv.at[p, me],
            send_sem=g_send.at[t], recv_sem=g_recv.at[p, me],
            device_id=(o // n_col, o % n_col), device_id_type=MESH,
        )

    def from_member(p, s):
        return pltpu.make_async_remote_copy(
            src_ref=gpart.at[0], dst_ref=grecv.at[p, s],
            send_sem=g_send.at[0], recv_sem=g_recv.at[p, s],
            device_id=(s // n_col, s % n_col), device_id_type=MESH,
        )

    def spread(p, o, s):
        t = p * n_dev + o
        return pltpu.make_async_remote_copy(
            src_ref=gfull.at[t], dst_ref=gfull.at[t],
            send_sem=f_send.at[p, s], recv_sem=f_recv.at[t],
            device_id=(s // n_col, s % n_col), device_id_type=MESH,
        )

    def each_peer(fn):
        def step(j, carry):
            fn((me + j) % n_dev)
            return carry
        lax.fori_loop(1, n_dev, step, 0)

    def owned(p, o, fn):
        if (p + 1) * n_dev <= pieces:
            fn()
        else:
            pl.when(p * n_dev + o < pieces)(fn)

    def each_owner(p, fn):
        each_peer(lambda o: owned(p, o, lambda: fn(o)))

    for p in range(passes):
        each_owner(p, lambda o, p=p: to_owner(p, o).start())

    for p in range(passes):
        def reduce_mine(p=p):
            t = p * n_dev + me
            grecv[p, me] = gpart[t]
            each_peer(lambda s: from_member(p, s).wait_recv())
            gfull[t] = jnp.sum(grecv[p], axis=0)
            each_peer(lambda s: spread(p, me, s).start())

        owned(p, me, reduce_mine)
    for p in range(passes):
        each_owner(p, lambda o, p=p: spread(p, o, me).wait_recv())

    mixed = gfull[each : 2 * each].reshape(half, half)
    below = jnp.where(rows > cols, mixed, 0.0)
    above = jnp.where(rows < cols, mixed, 0.0)
    gram[:half, :half] = jnp.where(
        rows == cols, jnp.broadcast_to(gfull[2 * each, 0:1, :], (half, half)), below + below.T
    )
    gram[:half, half:] = gfull[0:each].reshape(half, half)
    gram[half:, :half] = jnp.zeros((half, half), jnp.float32)
    gram[half:, half:] = jnp.where(rows == cols, mixed, above + above.T)

    for p in range(passes):
        each_owner(p, lambda o, p=p: to_owner(p, o).wait_send())
        owned(p, me, lambda p=p: each_peer(lambda s: spread(p, me, s).wait_send()))
    for k in range(2):
        for xp in order:
            for h in range(RS_CHUNKS):
                to_partner(k, xp, h).wait_send()
        for xp in order[:-1]:
            for h in range(RS_CHUNKS):
                across(k, xp, h, x).wait_send()

    def drain(i, carry):
        for needed, copy in hops(i // n_row, i % n_row):
            @pl.when(needed)
            def _(copy=copy):
                copy.wait_send()
        return carry

    lax.fori_loop(0, 2 * n_row, drain, 0)


def invert_factor(diag):
    n = diag.shape[0]
    lanes = 128
    rows = lax.broadcasted_iota(jnp.int32, (n, lanes), 0)
    cols = lax.broadcasted_iota(jnp.int32, (n, lanes), 1)
    eye = (cols - n == rows).astype(jnp.float32)
    work = jnp.concatenate([diag, eye[:, n:]], axis=1)
    scale = jnp.zeros((n, lanes), jnp.float32)
    for start in range(0, n, GROUP):
        picked = [
            jnp.broadcast_to(work[:, start + j : start + j + 1], (n, lanes))
            for j in range(GROUP)
        ]
        for j in range(GROUP):
            at = start + j
            pivot = picked[j][at : at + 1, :]
            root = lax.rsqrt(pivot)
            scale = jnp.where(rows == at, root, scale)
            weight = jnp.where(rows > at, picked[j] * (root * root), 0.0)
            for later in range(j + 1, GROUP):
                picked[later] = picked[later] - weight * picked[later][at : at + 1, :]
            work = work - weight * work[at : at + 1, :]
    return (work * scale)[:, n : 2 * n]


def factor_kernel(gram, panel, basis, upper, work):
    width = gram.shape[0]
    n = CHOL_BLOCK
    rows = lax.broadcasted_iota(jnp.int32, (width, width), 0)
    cols = lax.broadcasted_iota(jnp.int32, (width, width), 1)
    work[:, :width] = gram[...]
    work[:, width:] = (rows == cols).astype(jnp.float32)
    for start in range(0, width, n):
        stop = start + n
        inverse = invert_factor(work[start:stop, start:stop])
        done = jnp.dot(
            inverse, work[start:stop, :], precision=HIGH, preferred_element_type=jnp.float32
        )
        work[start:stop, :] = done
        if stop < width:
            work[stop:, :] -= lax.dot_general(
                done[:, stop:width], done, (((0,), (0,)), ((), ())),
                precision=HIGH, preferred_element_type=jnp.float32,
            )
    upper[...] = jnp.where(cols >= rows, work[:, :width], 0.0)
    basis[...] = lax.dot_general(
        panel[...], work[:, width:], (((1,), (1,)), ((), ())),
        precision=HIGH, preferred_element_type=jnp.float32,
    )


def on_device(n_row, n_col, vectors, tile_values, tile_row, tile_col, counts):
    slab, width = vectors.shape
    tiles = tile_values[0, 0]
    slots, block, _ = tiles.shape
    n_dev = n_row * n_col
    per_block = slab // block
    tile_rows, tile_cols = n_col * per_block, n_row * per_block
    number = jnp.arange(slots, dtype=jnp.int32)
    place = tile_row[0, 0] * tile_cols + tile_col[0, 0]
    place = jnp.where(number < counts[0, 0], place, -1)
    cell = jnp.arange(tile_rows * tile_cols, dtype=jnp.int32)
    table = jnp.min(jnp.where(cell[:, None] == place[None, :], number[None, :], slots), axis=1)
    half = width // 2
    pieces = 2 * (half // 8) + 1
    passes = pl.cdiv(pieces, n_dev)
    nx = n_col // 2
    vmem = pl.BlockSpec(memory_space=pltpu.VMEM)
    f32 = jnp.float32
    panel, gram = pl.pallas_call(
        functools.partial(panel_kernel, n_row, n_col),
        out_shape=(
            jax.ShapeDtypeStruct((slab, width), f32),
            jax.ShapeDtypeStruct((width, width), f32),
        ),
        in_specs=[
            pl.BlockSpec(memory_space=pltpu.SMEM),
            pl.BlockSpec(memory_space=pl.ANY),
            pl.BlockSpec(memory_space=pl.ANY),
        ],
        out_specs=(vmem, vmem),
        scratch_shapes=[
            pltpu.VMEM((2, n_row, slab, half), vectors.dtype),
            pltpu.VMEM((slots + 1, block, block), tiles.dtype),
            pltpu.VMEM((2, n_col, slab, half), f32),
            pltpu.VMEM((2, nx, slab, half), f32),
            pltpu.VMEM((2, nx, slab, half), f32),
            pltpu.VMEM((pieces, 8, half), f32),
            pltpu.VMEM((passes, n_dev, 8, half), f32),
            pltpu.VMEM((pieces, 8, half), f32),
            pltpu.SemaphoreType.DMA((TILE_DMAS,)),
            pltpu.SemaphoreType.DMA((2,)),
            pltpu.SemaphoreType.DMA((4, 2, n_row)),
            pltpu.SemaphoreType.DMA((2, n_row)),
            pltpu.SemaphoreType.DMA((2, nx, RS_CHUNKS)),
            pltpu.SemaphoreType.DMA((2, nx, RS_CHUNKS)),
            pltpu.SemaphoreType.DMA((2, nx, RS_CHUNKS)),
            pltpu.SemaphoreType.DMA((2, nx, RS_CHUNKS)),
            pltpu.SemaphoreType.DMA((pieces,)),
            pltpu.SemaphoreType.DMA((passes, n_dev)),
            pltpu.SemaphoreType.DMA((passes, n_dev)),
            pltpu.SemaphoreType.DMA((pieces,)),
        ],
        compiler_params=pltpu.CompilerParams(
            collective_id=0, has_side_effects=True, vmem_limit_bytes=56 << 20
        ),
        name="panel",
    )(table, vectors, tiles)
    basis, upper = pl.pallas_call(
        factor_kernel,
        out_shape=(
            jax.ShapeDtypeStruct((slab, width), f32),
            jax.ShapeDtypeStruct((width, width), f32),
        ),
        in_specs=[vmem, vmem],
        out_specs=(vmem, vmem),
        scratch_shapes=[pltpu.VMEM((width, 2 * width), f32)],
        name="factor",
    )(gram, panel)
    return (basis, upper)


def solution(mesh):
    n_row, n_col = mesh.shape["row"], mesh.shape["col"]
    return jax.shard_map(
        functools.partial(on_device, n_row, n_col),
        mesh=mesh,
        in_specs=(
            P(("row", "col"), None),
            P("row", "col", None, None, None),
            P("row", "col", None),
            P("row", "col", None),
            P("row", "col"),
        ),
        out_specs=(P(("row", "col"), None), P()),
        check_vma=False,
    )
```
